32 devices in a mesh: row: 4 (over y, x), query: 8 (over z, core).
Axes of the slice: x: 2, y: 2, z: 4, core: 2. Of those that a mesh axis runs over, the one named last changes fastest.
Arguments:
- logits: float32 [512, 1024], P('row'), may hold values from -9 to 309
- attributes: int32 [3, 16384], P(None, 'query'), may hold values from 0 to 63
- values: int32 [3, 16384], P(None, 'query'), may hold values from 0 to 15
- targets: float32 [16384], P('query'), may hold values from 0.25 to 1.75
Outputs:
- new_rows: float32 [512, 1024], P('row')
- residual: float32 [16384], P('query')
The draws below stay inside these ranges and needn't reach their ends.
All inputs are finite; a program needn't handle non-finite values.
Results may differ from the reference program's by a relative error of at most 0.0064.
Values sent between devices are 32-bit elements; how exact they have to be, the bound alone decides.
A program may use at most 64 MiB of HBM per device.

```python
import jax
import jax.numpy as jnp
from jax import lax

ATTRS = 64
VALS = 16
QDEV = 2048
COLS = 1024
ROWS = 512
QUERIES = 16384
N_QUERY = 8


def draw_logits(key, part):
    base_key = jax.random.fold_in(jax.random.fold_in(key, 17), 0)
    base = jnp.clip(1.5 * jax.random.normal(base_key, (ROWS, ATTRS, VALS), jnp.float32), -9.0, 9.0)
    return base.reshape(ROWS, ATTRS * VALS)


def plant(values, own_key, least, high):
    index_at = [jax.random.randint(jax.random.fold_in(own_key, axis), (), 0, length) for axis, length in enumerate(values.shape)]
    longest = values.shape.index(max(values.shape))
    neighbour = index_at[:longest] + [(index_at[longest] + 1) % values.shape[longest]] + index_at[longest + 1:]
    return values.at[tuple(index_at)].set(least).at[tuple(neighbour)].set(high)


def levels(key, shape, shards, least, high):
    level = 1.0
    for dim, shards_of in shards:
        heights = jax.random.uniform(jax.random.fold_in(jax.random.fold_in(key, 6), dim), (shards_of,), jnp.float32, least / len(shards), high / len(shards))
        level = level * jnp.repeat(jnp.exp(heights), shape[dim] // shards_of).reshape((-1,) + (1,) * (len(shape) - 1 - dim))
    return level


def setup_inputs(seed: int = 0) -> dict:
    key_of = jax.random.split(jax.random.key(seed), 5)
    return {
        "logits": draw_logits(jax.random.fold_in(key_of[4], 71), 0),
        "attributes": plant(jax.random.randint(key_of[1], (3, QUERIES), 0, ATTRS), jax.random.fold_in(key_of[1], 1), 0, ATTRS - 1).astype(jnp.int32),
        "values": plant(jax.random.randint(key_of[2], (3, QUERIES), 0, VALS), jax.random.fold_in(key_of[2], 1), 0, VALS - 1).astype(jnp.int32),
        "targets": jnp.clip(0.25 + 1.5 * jax.random.uniform(key_of[3], (QUERIES,), jnp.float32) ** levels(key_of[3], (QUERIES,), ((0, 8),), -0.2, 0.2), 0.25, 1.75),
    }


STEP_RATE = 2.0


def group_softmax(logit_rows):
    row_count = logit_rows.shape[0]
    grouped = logit_rows.reshape(row_count, -1, VALS)
    return jax.nn.softmax(grouped, axis=-1).reshape(row_count, -1)


def relaxed_update(logit_rows, relaxed, accumulated):
    row_count = logit_rows.shape[0]
    scaled = float(VALS * VALS) * accumulated
    grouped_p = relaxed.reshape(row_count, -1, VALS)
    grouped_d = scaled.reshape(row_count, -1, VALS)
    weighted_mean = jnp.sum(grouped_p * grouped_d, axis=-1, keepdims=True)
    tangent = (grouped_p * (grouped_d - weighted_mean)).reshape(row_count, -1)
    return group_softmax(logit_rows - STEP_RATE * tangent)


def reference(logits, attributes, values, targets):
    total_rows = logits.shape[0]
    relaxed = group_softmax(logits)
    relaxed_b = relaxed.astype(jnp.bfloat16)
    columns = (attributes * VALS + values).astype(jnp.int32)
    blocks = columns.reshape(3, N_QUERY, QDEV).transpose(1, 0, 2)
    answer_scale = float(VALS ** 3) / total_rows

    def forward(query_block):
        pick_one = relaxed_b[:, query_block[0]].astype(jnp.float32)
        pick_two = relaxed_b[:, query_block[1]].astype(jnp.float32)
        pick_three = relaxed_b[:, query_block[2]].astype(jnp.float32)
        return jnp.sum(pick_one * pick_two * pick_three, axis=0)

    answers = lax.map(forward, blocks).reshape(-1) * answer_scale
    residual = answers - targets

    def backward(running, inputs):
        query_block, misfit = inputs
        pick_one = relaxed_b[:, query_block[0]].astype(jnp.float32)
        pick_two = relaxed_b[:, query_block[1]].astype(jnp.float32)
        pick_three = relaxed_b[:, query_block[2]].astype(jnp.float32)
        weights = ((pick_two * pick_three) * misfit[None, :],
                   (pick_one * pick_three) * misfit[None, :],
                   (pick_one * pick_two) * misfit[None, :])
        for position in range(3):
            rounded = weights[position].astype(jnp.bfloat16).astype(jnp.float32)
            running = running + jax.ops.segment_sum(rounded.T, query_block[position], num_segments=COLS)
        return running, None

    start_value = jnp.zeros((COLS, total_rows), jnp.float32)
    accum_t, unused = lax.scan(backward, start_value, (blocks, residual.reshape(N_QUERY, QDEV)))
    new_rows = relaxed_update(logits, relaxed, accum_t.T)
    return new_rows, residual
```

```python
import functools

import jax
import jax.numpy as jnp
from jax import lax
from jax.experimental import pallas as pl
from jax.experimental.pallas import tpu as pltpu
from jax.sharding import PartitionSpec as P

VALS = 16
STEP_RATE = 2.0
CHUNK = 256
PARTS = 1
LOADS = 8
VMEM_BYTES = 48 * 1024 * 1024
LANES = 128
BLOCK = 256
PACK = 256
MESH = pl.DeviceIdType.MESH


def group_softmax(tall):
    cols, rows = tall.shape
    grouped = tall.reshape(cols // VALS, VALS, rows)
    shifted = jnp.exp(grouped - jnp.max(grouped, axis=1, keepdims=True))
    return (shifted / jnp.sum(shifted, axis=1, keepdims=True)).reshape(cols, rows)


def kernel(
    n_row, n_query, total_rows,
    log_hbm, att_hbm, val_hbm, tgt_hbm, gat, res_ref,
    log_v, att, val, tgt, log_t, rel_t, rel_b, sel, pair, wgt, ans, acc, sib, zin,
    load_sem, ans_send, ans_recv, send_sem, sib_recv, z_recv, ag_recv, fw_recv,
):
    me_r = lax.axis_index("row")
    me_q = lax.axis_index("query")
    me_z, core = me_q // 2, me_q % 2
    other = 1 - core
    n_z = n_query // 2
    rows, cols = log_hbm.shape
    queries = att.shape[1]
    half_q = queries // 2
    half_c = cols // 2
    share = half_c // n_z
    size = share // PARTS
    n_block = half_c // BLOCK
    lower = me_z < n_z // 2
    sibling = (me_r, me_z * 2 + other)

    def remote(src, dst, ssem, rsem, device):
        return pltpu.make_async_remote_copy(
            src_ref=src, dst_ref=dst, send_sem=ssem, recv_sem=rsem,
            device_id=device, device_id_type=MESH,
        )

    small = [
        pltpu.make_async_copy(att_hbm, att, load_sem.at[1]),
        pltpu.make_async_copy(val_hbm, val, load_sem.at[2]),
        pltpu.make_async_copy(tgt_hbm, tgt, load_sem.at[3]),
    ]
    band = rows // LOADS
    large = [
        pltpu.make_async_copy(
            log_hbm.at[b * band : (b + 1) * band], log_v.at[b * band : (b + 1) * band], load_sem.at[0]
        )
        for b in range(LOADS)
    ]
    for copy in large + small:
        copy.start()

    barrier = pltpu.get_barrier_semaphore()
    for d in range(1, n_row):
        pl.semaphore_signal(barrier, inc=1, device_id=(lax.rem(me_r + d, n_row), me_q), device_id_type=MESH)
    pl.semaphore_signal(barrier, inc=1, device_id=sibling, device_id_type=MESH)
    for d in range(1, n_z):
        pl.semaphore_signal(
            barrier, inc=1, device_id=(me_r, lax.rem(me_z + d, n_z) * 2 + core), device_id_type=MESH
        )

    pltpu.make_async_copy(log_hbm, log_v, load_sem.at[0]).wait()
    for b in range(cols // LANES):
        part = slice(b * LANES, (b + 1) * LANES)
        tall = log_v[:, part].T
        log_t[part, :] = tall
        relaxed = group_softmax(tall)
        rel_t[part, :] = relaxed
        side, inside = divmod(b * LANES, half_c)
        rel_b[side * rows : (side + 1) * rows, inside : inside + LANES] = relaxed.T.astype(jnp.bfloat16)
    for copy in small:
        copy.wait()

    places = lax.broadcasted_iota(jnp.int32, (PACK, CHUNK), 0).astype(jnp.float32).astype(jnp.bfloat16)
    one, zero = jnp.ones((), jnp.bfloat16), jnp.zeros((), jnp.bfloat16)
    chunks = half_q // CHUNK

    def ans_copy(h, d, slot):
        dst = (lax.rem(me_r + d, n_row), me_q)
        return remote(ans.at[h, slot], ans.at[h, slot], ans_send.at[h, d - 1], ans_recv.at[h, d - 1], dst)

    for h in range(2):

        def forward(c, carry, h=h):
            at = h * half_q + c * CHUNK
            base = at * 3
            picked = []
            for k in range(3):
                column = att[k : k + 1, pl.ds(at, CHUNK)] * VALS + val[k : k + 1, pl.ds(at, CHUNK)]
                high = column >= half_c
                low = jnp.where(high, column - half_c, column).astype(jnp.float32)
                parts = []
                for s in range(half_c // PACK):
                    index = jnp.broadcast_to(low - float(s * PACK), (PACK, CHUNK)).astype(jnp.bfloat16)
                    one_hot = jnp.where(places == index, one, zero)
                    sel[s * PACK : (s + 1) * PACK, pl.ds(base + k * CHUNK, CHUNK)] = one_hot
                    parts.append(one_hot)
                both = jnp.dot(rel_b[...], jnp.concatenate(parts, axis=0), preferred_element_type=jnp.float32)
                picked.append(jnp.where(high, both[rows:, :], both[:rows, :]))
            first = picked[0] * picked[1]
            pair[:, pl.ds(base, CHUNK)] = picked[1] * picked[2]
            pair[:, pl.ds(base + CHUNK, CHUNK)] = picked[0] * picked[2]
            pair[:, pl.ds(base + 2 * CHUNK, CHUNK)] = first
            partial = jnp.sum(first * picked[2], axis=0, keepdims=True)
            for i in range(CHUNK // LANES):
                ans[h, me_r, pl.ds(c * (CHUNK // LANES) + i, 1), :] = partial[:, i * LANES : (i + 1) * LANES]
            return carry

        for c in range(chunks):
            forward(c, 0)
        if h == 0:
            pl.semaphore_wait(barrier, n_row - 1 + n_z)
        for d in range(1, n_row):
            ans_copy(h, d, me_r).start()

    answer_scale = float(VALS**3) / total_rows
    half_lines = half_q // LANES

    def sums(block, h):
        span = slice(h * 3 * half_q, (h + 1) * 3 * half_q)
        return lax.dot_general(
            sel[block * BLOCK : (block + 1) * BLOCK, span], wgt[:, span], (((1,), (1,)), ((), ())),
            preferred_element_type=jnp.float32,
        )

    def at(p):
        return pl.ds(pl.multiple_of(p * size, size), size)

    def own(p):
        return pl.ds(pl.multiple_of(core * half_c + p * size, size), size)

    def theirs(p):
        return pl.ds(pl.multiple_of(other * half_c + p * size, size), size)

    def outward(i):
        return jnp.where(lower, n_z - 1 - i, i)

    def sib_copy(p):
        return remote(acc.at[0, other, at(p)], sib.at[at(p)], send_sem.at[0], sib_recv.at[p], sibling)

    def z_copy(part, dst_z, slot):
        return remote(
            acc.at[0, core, at(part * n_z + dst_z)], zin.at[part, slot], send_sem.at[1], z_recv.at[part, slot],
            (me_r, dst_z * 2 + core),
        )

    def ag_copy(part, dst_z, z):
        span = own(part * n_z + z)
        return remote(gat.at[span], gat.at[span], send_sem.at[2], ag_recv.at[part, z], (me_r, dst_z * 2 + core))

    def fw_copy(p, mine):
        span = own(p) if mine else theirs(p)
        return remote(gat.at[span], gat.at[span], send_sem.at[3], fw_recv.at[p], sibling)

    def toward(d):
        return lax.rem(me_z + jnp.where(lower, 1, n_z - 1) * d, n_z)

    def spread(part):
        for i in range(n_z):
            z = outward(i)
            p = part * n_z + z
            sib_copy(p).wait_recv()
            summed = acc[0, core, at(p)] + sib[at(p)]

            @pl.when(z != me_z)
            def _():
                acc[0, core, at(p)] = summed
                z_copy(part, z, me_z).start()

            @pl.when(z == me_z)
            def _():
                zin[part, me_z] = summed

    def reduce(part):
        for d in range(1, n_z):
            z_copy(part, me_z, lax.rem(me_z + d, n_z)).wait_recv()
        accumulated = zin[part, 0]
        for z in range(1, n_z):
            accumulated = accumulated + zin[part, z]
        mine = own(part * n_z + me_z)
        groups = size // VALS
        grouped_d = (float(VALS * VALS) * accumulated).reshape(groups, VALS, rows)
        grouped_p = rel_t[mine, :].reshape(groups, VALS, rows)
        weighted_mean = jnp.sum(grouped_p * grouped_d, axis=1, keepdims=True)
        tangent = (grouped_p * (grouped_d - weighted_mean)).reshape(size, rows)
        gat[mine, :] = group_softmax(log_t[mine, :] - STEP_RATE * tangent)
        for d in range(n_z - 1, 0, -1):
            ag_copy(part, toward(d), me_z).start()
        fw_copy(part * n_z + me_z, True).start()

    def relay(part):
        for d in range(1, n_z):
            z = toward(d)
            ag_copy(part, z, z).wait_recv()
            fw_copy(part * n_z + z, True).start()

    for h in range(2):
        for d in range(1, n_row):
            ans_copy(h, d, lax.rem(me_r + n_row - d, n_row)).wait_recv()
        total = ans[h, 0]
        for r in range(1, n_row):
            total = total + ans[h, r]
        lines = slice(h * half_lines, (h + 1) * half_lines)
        residual = total * answer_scale - tgt[lines, :]
        res_ref[lines, :] = residual
        for line in range(half_lines):
            chunk, inside = divmod(line * LANES, CHUNK)
            misfit = residual[line : line + 1, :]
            for k in range(3):
                start = h * 3 * half_q + (chunk * 3 + k) * CHUNK + inside
                span = slice(start, start + LANES)
                query = h * half_q + line * LANES
                high = att[k : k + 1, query : query + LANES] >= half_c // VALS
                product = pair[:, span]
                wgt[:rows, span] = (product * jnp.where(high, 0.0, misfit)).astype(jnp.bfloat16)
                wgt[rows:, span] = (product * jnp.where(high, misfit, 0.0)).astype(jnp.bfloat16)
        for block in range(n_block):
            found = sums(block, h)
            span = slice(block * BLOCK, (block + 1) * BLOCK)
            acc[h, 0, span] = found[:, :rows]
            acc[h, 1, span] = found[:, rows:]
    for side in range(2):
        acc[0, side] = acc[0, side] + acc[1, side]
    for part in range(PARTS):
        for i in range(n_z):
            sib_copy(part * n_z + outward(i)).start()
    for part in range(PARTS):
        spread(part)
    for part in range(PARTS):
        reduce(part)
    for part in range(PARTS):
        relay(part)
    for part in range(PARTS):
        for d in range(n_z):
            fw_copy(part * n_z + toward(d), False).wait_recv()

    for h in range(2):
        for d in range(1, n_row):
            ans_copy(h, d, me_r).wait_send()

    def sent(many, sem):
        span = pl.ds(0, many * share)
        remote(acc.at[0, 0, span], acc.at[0, 0, span], send_sem.at[sem], sib_recv.at[0], sibling).wait_send()

    sent(n_z, 0)
    sent(n_z - 1, 1)
    sent(n_z - 1, 2)
    sent(n_z, 3)

def finish(tall_ref, misfit_ref, new_ref, res_ref):
    for b in range(tall_ref.shape[0] // LANES):
        part = slice(b * LANES, (b + 1) * LANES)
        new_ref[:, part] = tall_ref[part, :].T
    res_ref[...] = misfit_ref[...]


def local(n_row, n_query, logits, attributes, values, targets):
    rows, cols = logits.shape
    queries = attributes.shape[1]
    half_c = cols // 2
    n_z = n_query // 2
    n_piece = n_z * PARTS
    dma = pltpu.SemaphoreType.DMA
    vmem = pl.BlockSpec(memory_space=pltpu.VMEM)
    hbm = pl.BlockSpec(memory_space=pltpu.HBM)
    f32, bf16 = jnp.float32, jnp.bfloat16
    given = (logits, attributes, values, targets.reshape(queries // LANES, LANES))
    tall, misfit = pl.pallas_call(
        functools.partial(kernel, n_row, n_query, rows * n_row),
        out_shape=(
            jax.ShapeDtypeStruct((cols, rows), f32),
            jax.ShapeDtypeStruct((queries // LANES, LANES), f32),
        ),
        in_specs=[hbm] * 4,
        out_specs=(vmem, vmem),
        scratch_shapes=[
            pltpu.VMEM((rows, cols), f32),
            pltpu.VMEM((3, queries), jnp.int32),
            pltpu.VMEM((3, queries), jnp.int32),
            pltpu.VMEM((queries // LANES, LANES), f32),
            pltpu.VMEM((cols, rows), f32),
            pltpu.VMEM((cols, rows), f32),
            pltpu.VMEM((2 * rows, half_c), bf16),
            pltpu.VMEM((half_c, 3 * queries), bf16),
            pltpu.VMEM((rows, 3 * queries), f32),
            pltpu.VMEM((2 * rows, 3 * queries), bf16),
            pltpu.VMEM((2, n_row, queries // 2 // LANES, LANES), f32),
            pltpu.VMEM((2, 2, half_c, rows), f32),
            pltpu.VMEM((half_c, rows), f32),
            pltpu.VMEM((PARTS, n_z, half_c // n_piece, rows), f32),
            dma((4,)), dma((2, n_row - 1)), dma((2, n_row - 1)), dma((4,)),
            dma((n_piece,)), dma((PARTS, n_z)), dma((PARTS, n_z)), dma((n_piece,)),
        ],
        compiler_params=pltpu.CompilerParams(
            collective_id=0, has_side_effects=True, vmem_limit_bytes=VMEM_BYTES
        ),
    )(*(pltpu.with_memory_space_constraint(a, pltpu.HBM) for a in given))
    new_rows, residual = pl.pallas_call(
        finish,
        out_shape=(
            jax.ShapeDtypeStruct((rows, cols), jnp.float32),
            jax.ShapeDtypeStruct((queries // LANES, LANES), jnp.float32),
        ),
        in_specs=[vmem, vmem],
        out_specs=(vmem, vmem),
        compiler_params=pltpu.CompilerParams(vmem_limit_bytes=4 * 1024 * 1024),
    )(tall, misfit)
    return new_rows, residual.reshape(queries)


def solution(mesh):
    placed = (P("row", None), P(None, "query"), P(None, "query"), P("query"))
    return jax.shard_map(
        functools.partial(local, mesh.shape["row"], mesh.shape["query"]),
        mesh=mesh, in_specs=placed, out_specs=(P("row", None), P("query")), check_vma=False,
    )
```

```python
import functools

import jax
import jax.numpy as jnp
from jax import lax
from jax.experimental import pallas as pl
from jax.experimental.pallas import tpu as pltpu
from jax.sharding import PartitionSpec as P

VALS = 16
STEP_RATE = 2.0
CHUNK = 256
PARTS = 2
LOADS = 8
VMEM_BYTES = 48 * 1024 * 1024
LANES = 128
BLOCK = 256
PACK = 256
MESH = pl.DeviceIdType.MESH


def group_softmax(tall):
    cols, rows = tall.shape
    grouped = tall.reshape(cols // VALS, VALS, rows)
    shifted = jnp.exp(grouped - jnp.max(grouped, axis=1, keepdims=True))
    return (shifted / jnp.sum(shifted, axis=1, keepdims=True)).reshape(cols, rows)


def kernel(
    n_row, n_query, total_rows,
    log_hbm, att_hbm, val_hbm, tgt_hbm, gat, res_ref,
    log_v, att, val, tgt, log_t, rel_t, rel_b, sel, pair, wgt, ans, acc, sib, zin,
    load_sem, ans_send, ans_recv, send_sem, sib_recv, z_recv, ag_recv, fw_recv,
):
    me_r = lax.axis_index("row")
    me_q = lax.axis_index("query")
    me_z, core = me_q // 2, me_q % 2
    other = 1 - core
    n_z = n_query // 2
    rows, cols = log_hbm.shape
    queries = att.shape[1]
    half_q = queries // 2
    half_c = cols // 2
    share = half_c // n_z
    size = share // PARTS
    n_block = half_c // BLOCK
    lower = me_z < n_z // 2
    sibling = (me_r, me_z * 2 + other)

    def remote(src, dst, ssem, rsem, device):
        return pltpu.make_async_remote_copy(
            src_ref=src, dst_ref=dst, send_sem=ssem, recv_sem=rsem,
            device_id=device, device_id_type=MESH,
        )

    small = [
        pltpu.make_async_copy(att_hbm, att, load_sem.at[1]),
        pltpu.make_async_copy(val_hbm, val, load_sem.at[2]),
        pltpu.make_async_copy(tgt_hbm, tgt, load_sem.at[3]),
    ]
    band = rows // LOADS
    large = [
        pltpu.make_async_copy(
            log_hbm.at[b * band : (b + 1) * band], log_v.at[b * band : (b + 1) * band], load_sem.at[0]
        )
        for b in range(LOADS)
    ]
    for copy in large + small:
        copy.start()

    barrier = pltpu.get_barrier_semaphore()
    for d in range(1, n_row):
        pl.semaphore_signal(barrier, inc=1, device_id=(lax.rem(me_r + d, n_row), me_q), device_id_type=MESH)
    pl.semaphore_signal(barrier, inc=1, device_id=sibling, device_id_type=MESH)
    for d in range(1, n_z):
        pl.semaphore_signal(
            barrier, inc=1, device_id=(me_r, lax.rem(me_z + d, n_z) * 2 + core), device_id_type=MESH
        )

    pltpu.make_async_copy(log_hbm, log_v, load_sem.at[0]).wait()
    for b in range(cols // LANES):
        part = slice(b * LANES, (b + 1) * LANES)
        tall = log_v[:, part].T
        log_t[part, :] = tall
        relaxed = group_softmax(tall)
        rel_t[part, :] = relaxed
        side, inside = divmod(b * LANES, half_c)
        rel_b[side * rows : (side + 1) * rows, inside : inside + LANES] = relaxed.T.astype(jnp.bfloat16)
    for copy in small:
        copy.wait()

    places = lax.broadcasted_iota(jnp.int32, (PACK, CHUNK), 0).astype(jnp.float32).astype(jnp.bfloat16)
    one, zero = jnp.ones((), jnp.bfloat16), jnp.zeros((), jnp.bfloat16)
    chunks = half_q // CHUNK

    def ans_copy(h, d, slot):
        dst = (lax.rem(me_r + d, n_row), me_q)
        return remote(ans.at[h, slot], ans.at[h, slot], ans_send.at[h, d - 1], ans_recv.at[h, d - 1], dst)

    for h in range(2):

        def forward(c, carry, h=h):
            at = h * half_q + c * CHUNK
            base = at * 3
            picked = []
            for k in range(3):
                column = att[k : k + 1, pl.ds(at, CHUNK)] * VALS + val[k : k + 1, pl.ds(at, CHUNK)]
                high = column >= half_c
                low = jnp.where(high, column - half_c, column).astype(jnp.float32)
                parts = []
                for s in range(half_c // PACK):
                    index = jnp.broadcast_to(low - float(s * PACK), (PACK, CHUNK)).astype(jnp.bfloat16)
                    one_hot = jnp.where(places == index, one, zero)
                    sel[s * PACK : (s + 1) * PACK, pl.ds(base + k * CHUNK, CHUNK)] = one_hot
                    parts.append(one_hot)
                both = jnp.dot(rel_b[...], jnp.concatenate(parts, axis=0), preferred_element_type=jnp.float32)
                picked.append(jnp.where(high, both[rows:, :], both[:rows, :]))
            first = picked[0] * picked[1]
            pair[:, pl.ds(base, CHUNK)] = picked[1] * picked[2]
            pair[:, pl.ds(base + CHUNK, CHUNK)] = picked[0] * picked[2]
            pair[:, pl.ds(base + 2 * CHUNK, CHUNK)] = first
            partial = jnp.sum(first * picked[2], axis=0, keepdims=True)
            for i in range(CHUNK // LANES):
                ans[h, me_r, pl.ds(c * (CHUNK // LANES) + i, 1), :] = partial[:, i * LANES : (i + 1) * LANES]
            return carry

        for c in range(chunks):
            forward(c, 0)
        if h == 0:
            pl.semaphore_wait(barrier, n_row - 1 + n_z)
        for d in range(1, n_row):
            ans_copy(h, d, me_r).start()

    answer_scale = float(VALS**3) / total_rows
    half_lines = half_q // LANES

    def sums(block, h):
        span = slice(h * 3 * half_q, (h + 1) * 3 * half_q)
        return lax.dot_general(
            sel[block * BLOCK : (block + 1) * BLOCK, span], wgt[:, span], (((1,), (1,)), ((), ())),
            preferred_element_type=jnp.float32,
        )

    def at(p):
        return pl.ds(pl.multiple_of(p * size, size), size)

    def own(p):
        return pl.ds(pl.multiple_of(core * half_c + p * size, size), size)

    def theirs(p):
        return pl.ds(pl.multiple_of(other * half_c + p * size, size), size)

    def outward(i):
        return i

    def sib_copy(p):
        return remote(acc.at[0, other, at(p)], sib.at[at(p)], send_sem.at[0], sib_recv.at[p], sibling)

    def z_copy(part, dst_z, slot):
        return remote(
            acc.at[0, core, at(part * n_z + dst_z)], zin.at[part, slot], send_sem.at[1], z_recv.at[part, slot],
            (me_r, dst_z * 2 + core),
        )

    def ag_copy(part, dst_z, z):
        span = own(part * n_z + z)
        return remote(gat.at[span], gat.at[span], send_sem.at[2], ag_recv.at[part, z], (me_r, dst_z * 2 + core))

    def fw_copy(p, mine):
        span = own(p) if mine else theirs(p)
        return remote(gat.at[span], gat.at[span], send_sem.at[3], fw_recv.at[p], sibling)

    def toward(d):
        return lax.rem(me_z + jnp.where(lower, 1, n_z - 1) * d, n_z)

    def spread(part):
        for i in range(n_z):
            z = outward(i)
            p = part * n_z + z
            sib_copy(p).wait_recv()
            summed = acc[0, core, at(p)] + sib[at(p)]

            @pl.when(z != me_z)
            def _():
                acc[0, core, at(p)] = summed
                z_copy(part, z, me_z).start()

            @pl.when(z == me_z)
            def _():
                zin[part, me_z] = summed

    def reduce(part):
        for d in range(1, n_z):
            z_copy(part, me_z, lax.rem(me_z + d, n_z)).wait_recv()
        accumulated = zin[part, 0]
        for z in range(1, n_z):
            accumulated = accumulated + zin[part, z]
        mine = own(part * n_z + me_z)
        groups = size // VALS
        grouped_d = (float(VALS * VALS) * accumulated).reshape(groups, VALS, rows)
        grouped_p = rel_t[mine, :].reshape(groups, VALS, rows)
        weighted_mean = jnp.sum(grouped_p * grouped_d, axis=1, keepdims=True)
        tangent = (grouped_p * (grouped_d - weighted_mean)).reshape(size, rows)
        gat[mine, :] = group_softmax(log_t[mine, :] - STEP_RATE * tangent)
        for z in range(n_z):
            @pl.when(z != me_z)
            def _():
                ag_copy(part, z, me_z).start()
        fw_copy(part * n_z + me_z, True).start()

    def relay(part):
        for d in range(1, n_z):
            z = toward(d)
            ag_copy(part, z, z).wait_recv()
            fw_copy(part * n_z + z, True).start()

    for h in range(2):
        for d in range(1, n_row):
            ans_copy(h, d, lax.rem(me_r + n_row - d, n_row)).wait_recv()
        total = ans[h, 0]
        for r in range(1, n_row):
            total = total + ans[h, r]
        lines = slice(h * half_lines, (h + 1) * half_lines)
        residual = total * answer_scale - tgt[lines, :]
        res_ref[lines, :] = residual
        for line in range(half_lines):
            chunk, inside = divmod(line * LANES, CHUNK)
            misfit = residual[line : line + 1, :]
            for k in range(3):
                start = h * 3 * half_q + (chunk * 3 + k) * CHUNK + inside
                span = slice(start, start + LANES)
                query = h * half_q + line * LANES
                high = att[k : k + 1, query : query + LANES] >= half_c // VALS
                product = pair[:, span]
                wgt[:rows, span] = (product * jnp.where(high, 0.0, misfit)).astype(jnp.bfloat16)
                wgt[rows:, span] = (product * jnp.where(high, misfit, 0.0)).astype(jnp.bfloat16)
        for block in range(n_block):
            found = sums(block, h)
            span = slice(block * BLOCK, (block + 1) * BLOCK)
            acc[h, 0, span] = found[:, :rows]
            acc[h, 1, span] = found[:, rows:]
    for side in range(2):
        acc[0, side] = acc[0, side] + acc[1, side]
    for part in range(PARTS):
        for i in range(n_z):
            sib_copy(part * n_z + outward(i)).start()
    for part in range(PARTS):
        spread(part)
    for part in range(PARTS):
        reduce(part)
    for part in range(PARTS):
        relay(part)
    for part in range(PARTS):
        for d in range(n_z):
            fw_copy(part * n_z + toward(d), False).wait_recv()

    for h in range(2):
        for d in range(1, n_row):
            ans_copy(h, d, me_r).wait_send()

    def sent(many, sem):
        span = pl.ds(0, many * share)
        remote(acc.at[0, 0, span], acc.at[0, 0, span], send_sem.at[sem], sib_recv.at[0], sibling).wait_send()

    sent(n_z, 0)
    sent(n_z - 1, 1)
    sent(n_z - 1, 2)
    sent(n_z, 3)

def finish(tall_ref, misfit_ref, new_ref, res_ref):
    for b in range(tall_ref.shape[0] // LANES):
        part = slice(b * LANES, (b + 1) * LANES)
        new_ref[:, part] = tall_ref[part, :].T
    res_ref[...] = misfit_ref[...]


def local(n_row, n_query, logits, attributes, values, targets):
    rows, cols = logits.shape
    queries = attributes.shape[1]
    half_c = cols // 2
    n_z = n_query // 2
    n_piece = n_z * PARTS
    dma = pltpu.SemaphoreType.DMA
    vmem = pl.BlockSpec(memory_space=pltpu.VMEM)
    hbm = pl.BlockSpec(memory_space=pltpu.HBM)
    f32, bf16 = jnp.float32, jnp.bfloat16
    given = (logits, attributes, values, targets.reshape(queries // LANES, LANES))
    tall, misfit = pl.pallas_call(
        functools.partial(kernel, n_row, n_query, rows * n_row),
        out_shape=(
            jax.ShapeDtypeStruct((cols, rows), f32),
            jax.ShapeDtypeStruct((queries // LANES, LANES), f32),
        ),
        in_specs=[hbm] * 4,
        out_specs=(vmem, vmem),
        scratch_shapes=[
            pltpu.VMEM((rows, cols), f32),
            pltpu.VMEM((3, queries), jnp.int32),
            pltpu.VMEM((3, queries), jnp.int32),
            pltpu.VMEM((queries // LANES, LANES), f32),
            pltpu.VMEM((cols, rows), f32),
            pltpu.VMEM((cols, rows), f32),
            pltpu.VMEM((2 * rows, half_c), bf16),
            pltpu.VMEM((half_c, 3 * queries), bf16),
            pltpu.VMEM((rows, 3 * queries), f32),
            pltpu.VMEM((2 * rows, 3 * queries), bf16),
            pltpu.VMEM((2, n_row, queries // 2 // LANES, LANES), f32),
            pltpu.VMEM((2, 2, half_c, rows), f32),
            pltpu.VMEM((half_c, rows), f32),
            pltpu.VMEM((PARTS, n_z, half_c // n_piece, rows), f32),
            dma((4,)), dma((2, n_row - 1)), dma((2, n_row - 1)), dma((4,)),
            dma((n_piece,)), dma((PARTS, n_z)), dma((PARTS, n_z)), dma((n_piece,)),
        ],
        compiler_params=pltpu.CompilerParams(
            collective_id=0, has_side_effects=True, vmem_limit_bytes=VMEM_BYTES
        ),
    )(*(pltpu.with_memory_space_constraint(a, pltpu.HBM) for a in given))
    new_rows, residual = pl.pallas_call(
        finish,
        out_shape=(
            jax.ShapeDtypeStruct((rows, cols), jnp.float32),
            jax.ShapeDtypeStruct((queries // LANES, LANES), jnp.float32),
        ),
        in_specs=[vmem, vmem],
        out_specs=(vmem, vmem),
        compiler_params=pltpu.CompilerParams(vmem_limit_bytes=4 * 1024 * 1024),
    )(tall, misfit)
    return new_rows, residual.reshape(queries)


def solution(mesh):
    placed = (P("row", None), P(None, "query"), P(None, "query"), P("query"))
    return jax.shard_map(
        functools.partial(local, mesh.shape["row"], mesh.shape["query"]),
        mesh=mesh, in_specs=placed, out_specs=(P("row", None), P("query")), check_vma=False,
    )
```

```python
import functools

import jax
import jax.numpy as jnp
from jax import lax
from jax.experimental import pallas as pl
from jax.experimental.pallas import tpu as pltpu
from jax.sharding import PartitionSpec as P

VALS = 16
STEP_RATE = 2.0
CHUNK = 256
PARTS = 2
LOADS = 4
VMEM_BYTES = 48 * 1024 * 1024
LANES = 128
BLOCK = 256
PACK = 256
MESH = pl.DeviceIdType.MESH


def group_softmax(tall):
    cols, rows = tall.shape
    grouped = tall.reshape(cols // VALS, VALS, rows)
    shifted = jnp.exp(grouped - jnp.max(grouped, axis=1, keepdims=True))
    return (shifted / jnp.sum(shifted, axis=1, keepdims=True)).reshape(cols, rows)


def kernel(
    n_row, n_query, total_rows,
    log_hbm, att_hbm, val_hbm, tgt_hbm, gat, res_ref,
    log_v, att, val, tgt, log_t, rel_t, rel_b, sel, pair, wgt, ans, acc, sib, zin,
    load_sem, ans_recv, send_sem, sib_recv, z_recv, ag_recv, fw_recv,
):
    me_r = lax.axis_index("row")
    me_q = lax.axis_index("query")
    me_z, core = me_q // 2, me_q % 2
    other = 1 - core
    n_z = n_query // 2
    rows, cols = log_hbm.shape
    queries = att.shape[1]
    half_q = queries // 2
    half_c = cols // 2
    share = half_c // n_z
    size = share // PARTS
    n_block = half_c // BLOCK
    lower = me_z < n_z // 2
    sibling = (me_r, me_z * 2 + other)

    def remote(src, dst, ssem, rsem, device):
        return pltpu.make_async_remote_copy(
            src_ref=src, dst_ref=dst, send_sem=ssem, recv_sem=rsem,
            device_id=device, device_id_type=MESH,
        )

    small = [
        pltpu.make_async_copy(att_hbm, att, load_sem.at[2]),
        pltpu.make_async_copy(val_hbm, val, load_sem.at[3]),
        pltpu.make_async_copy(tgt_hbm, tgt, load_sem.at[4]),
    ]
    band = rows // LOADS
    wide = cols // 2
    large = [
        pltpu.make_async_copy(
            log_hbm.at[b * band : (b + 1) * band, side * wide : (side + 1) * wide],
            log_v.at[b * band : (b + 1) * band, side * wide : (side + 1) * wide], load_sem.at[side],
        )
        for side in range(2) for b in range(LOADS)
    ]
    for copy in large + small:
        copy.start()

    barrier = pltpu.get_barrier_semaphore()
    for d in range(1, n_row):
        pl.semaphore_signal(barrier, inc=1, device_id=(lax.rem(me_r + d, n_row), me_q), device_id_type=MESH)
    pl.semaphore_signal(barrier, inc=1, device_id=sibling, device_id_type=MESH)
    for d in range(1, n_z):
        pl.semaphore_signal(
            barrier, inc=1, device_id=(me_r, lax.rem(me_z + d, n_z) * 2 + core), device_id_type=MESH
        )

    for b in range(cols // LANES):
        if b * LANES % wide == 0:
            side = b * LANES // wide
            half_v = log_v.at[:, side * wide : (side + 1) * wide]
            pltpu.make_async_copy(half_v, half_v, load_sem.at[side]).wait()
        part = slice(b * LANES, (b + 1) * LANES)
        tall = log_v[:, part].T
        log_t[part, :] = tall
        relaxed = group_softmax(tall)
        rel_t[part, :] = relaxed
        side, inside = divmod(b * LANES, half_c)
        rel_b[side * rows : (side + 1) * rows, inside : inside + LANES] = relaxed.T.astype(jnp.bfloat16)
    for copy in small:
        copy.wait()

    places = lax.broadcasted_iota(jnp.int32, (PACK, CHUNK), 0).astype(jnp.float32).astype(jnp.bfloat16)
    one, zero = jnp.ones((), jnp.bfloat16), jnp.zeros((), jnp.bfloat16)
    chunks = half_q // CHUNK

    def ans_copy(h, d, slot):
        dst = (lax.rem(me_r + d, n_row), me_q)
        return remote(ans.at[h, slot], ans.at[h, slot], send_sem.at[4], ans_recv.at[h], dst)

    for h in range(2):

        def forward(c, carry, h=h):
            at = h * half_q + c * CHUNK
            base = at * 3
            picked = []
            for k in range(3):
                column = att[k : k + 1, pl.ds(at, CHUNK)] * VALS + val[k : k + 1, pl.ds(at, CHUNK)]
                high = column >= half_c
                low = jnp.where(high, column - half_c, column).astype(jnp.float32)
                parts = []
                for s in range(half_c // PACK):
                    index = jnp.broadcast_to(low - float(s * PACK), (PACK, CHUNK)).astype(jnp.bfloat16)
                    one_hot = jnp.where(places == index, one, zero)
                    sel[s * PACK : (s + 1) * PACK, pl.ds(base + k * CHUNK, CHUNK)] = one_hot
                    parts.append(one_hot)
                both = jnp.dot(rel_b[...], jnp.concatenate(parts, axis=0), preferred_element_type=jnp.float32)
                picked.append(jnp.where(high, both[rows:, :], both[:rows, :]))
            first = picked[0] * picked[1]
            pair[:, pl.ds(base, CHUNK)] = picked[1] * picked[2]
            pair[:, pl.ds(base + CHUNK, CHUNK)] = picked[0] * picked[2]
            pair[:, pl.ds(base + 2 * CHUNK, CHUNK)] = first
            partial = jnp.sum(first * picked[2], axis=0, keepdims=True)
            for i in range(CHUNK // LANES):
                ans[h, me_r, pl.ds(c * (CHUNK // LANES) + i, 1), :] = partial[:, i * LANES : (i + 1) * LANES]
            return carry

        for c in range(chunks):
            forward(c, 0)
        if h == 0:
            pl.semaphore_wait(barrier, n_row - 1 + n_z)
        for d in range(1, n_row):
            ans_copy(h, d, me_r).start()

    answer_scale = float(VALS**3) / total_rows
    half_lines = half_q // LANES

    def sums(block, h):
        span = slice(h * 3 * half_q, (h + 1) * 3 * half_q)
        return lax.dot_general(
            sel[block * BLOCK : (block + 1) * BLOCK, span], wgt[:, span], (((1,), (1,)), ((), ())),
            preferred_element_type=jnp.float32,
        )

    def at(p):
        return pl.ds(pl.multiple_of(p * size, size), size)

    def own(p):
        return pl.ds(pl.multiple_of(core * half_c + p * size, size), size)

    def theirs(p):
        return pl.ds(pl.multiple_of(other * half_c + p * size, size), size)

    def outward(i):
        return i

    def sib_copy(p):
        return remote(acc.at[0, other, at(p)], sib.at[at(p)], send_sem.at[0], sib_recv.at[p], sibling)

    def z_copy(part, dst_z, slot):
        return remote(
            acc.at[0, core, at(part * n_z + dst_z)], zin.at[part, slot], send_sem.at[1], z_recv.at[part],
            (me_r, dst_z * 2 + core),
        )

    def ag_copy(part, dst_z, z):
        span = own(part * n_z + z)
        return remote(gat.at[span], gat.at[span], send_sem.at[2], ag_recv.at[part, z], (me_r, dst_z * 2 + core))

    def fw_copy(p, mine):
        span = own(p) if mine else theirs(p)
        return remote(gat.at[span], gat.at[span], send_sem.at[3], fw_recv.at[0], sibling)

    def toward(d):
        return lax.rem(me_z + jnp.where(lower, 1, n_z - 1) * d, n_z)

    def spread(part):
        for i in range(n_z):
            z = outward(i)
            p = part * n_z + z
            sib_copy(p).wait_recv()
            summed = acc[0, core, at(p)] + sib[at(p)]

            @pl.when(z != me_z)
            def _():
                acc[0, core, at(p)] = summed
                z_copy(part, z, me_z).start()

            @pl.when(z == me_z)
            def _():
                zin[part, me_z] = summed

    def reduce(part):
        remote(zin.at[part, 1:], zin.at[part, 1:], send_sem.at[1], z_recv.at[part], sibling).wait_recv()
        accumulated = zin[part, 0]
        for z in range(1, n_z):
            accumulated = accumulated + zin[part, z]
        mine = own(part * n_z + me_z)
        groups = size // VALS
        grouped_d = (float(VALS * VALS) * accumulated).reshape(groups, VALS, rows)
        grouped_p = rel_t[mine, :].reshape(groups, VALS, rows)
        weighted_mean = jnp.sum(grouped_p * grouped_d, axis=1, keepdims=True)
        tangent = (grouped_p * (grouped_d - weighted_mean)).reshape(size, rows)
        gat[mine, :] = group_softmax(log_t[mine, :] - STEP_RATE * tangent)
        @pl.when(me_z != 0)
        def _():
            ag_copy(part, 0, me_z).start()

        @pl.when(me_z == 0)
        def _():
            for z in range(1, n_z):
                ag_copy(part, z, 0).start()

        fw_copy(part * n_z + me_z, True).start()

    def relay(part):
        for d in range(1, n_z):
            z = toward(d)
            ag_copy(part, z, z).wait_recv()
            fw_copy(part * n_z + z, True).start()

    for h in range(2):
        remote(ans.at[h, 1:], ans.at[h, 1:], send_sem.at[4], ans_recv.at[h], sibling).wait_recv()
        total = ans[h, 0]
        for r in range(1, n_row):
            total = total + ans[h, r]
        lines = slice(h * half_lines, (h + 1) * half_lines)
        residual = total * answer_scale - tgt[lines, :]
        res_ref[lines, :] = residual
        for line in range(half_lines):
            chunk, inside = divmod(line * LANES, CHUNK)
            misfit = residual[line : line + 1, :]
            for k in range(3):
                start = h * 3 * half_q + (chunk * 3 + k) * CHUNK + inside
                span = slice(start, start + LANES)
                query = h * half_q + line * LANES
                high = att[k : k + 1, query : query + LANES] >= half_c // VALS
                product = pair[:, span]
                wgt[:rows, span] = (product * jnp.where(high, 0.0, misfit)).astype(jnp.bfloat16)
                wgt[rows:, span] = (product * jnp.where(high, misfit, 0.0)).astype(jnp.bfloat16)
        for block in range(n_block):
            found = sums(block, h)
            span = slice(block * BLOCK, (block + 1) * BLOCK)
            acc[h, 0, span] = found[:, :rows]
            acc[h, 1, span] = found[:, rows:]
    for side in range(2):
        acc[0, side] = acc[0, side] + acc[1, side]
    for part in range(PARTS):
        for i in range(n_z):
            sib_copy(part * n_z + outward(i)).start()
    for part in range(PARTS):
        spread(part)
    for part in range(PARTS):
        reduce(part)
    for part in range(PARTS):
        for z in range(1, n_z):
            @pl.when(jnp.logical_and(me_z != 0, z != me_z))
            def _():
                ag_copy(part, z, me_z).start()
    for part in range(PARTS):
        relay(part)
    half = gat.at[pl.ds(0, half_c)]
    remote(half, half, send_sem.at[3], fw_recv.at[0], sibling).wait_recv()

    remote(ans.at[:, 1:], ans.at[:, 1:], send_sem.at[4], ans_recv.at[0], sibling).wait_send()

    def sent(many, sem):
        span = pl.ds(0, many * share)
        remote(acc.at[0, 0, span], acc.at[0, 0, span], send_sem.at[sem], sib_recv.at[0], sibling).wait_send()

    sent(n_z, 0)
    sent(n_z - 1, 1)
    sent(n_z - 1, 2)
    sent(n_z, 3)

def finish(tall_ref, misfit_ref, new_ref, res_ref):
    for b in range(tall_ref.shape[0] // LANES):
        part = slice(b * LANES, (b + 1) * LANES)
        new_ref[:, part] = tall_ref[part, :].T
    res_ref[...] = misfit_ref[...]


def local(n_row, n_query, logits, attributes, values, targets):
    rows, cols = logits.shape
    queries = attributes.shape[1]
    half_c = cols // 2
    n_z = n_query // 2
    n_piece = n_z * PARTS
    dma = pltpu.SemaphoreType.DMA
    vmem = pl.BlockSpec(memory_space=pltpu.VMEM)
    hbm = pl.BlockSpec(memory_space=pltpu.HBM)
    f32, bf16 = jnp.float32, jnp.bfloat16
    given = (logits, attributes, values, targets.reshape(queries // LANES, LANES))
    tall, misfit = pl.pallas_call(
        functools.partial(kernel, n_row, n_query, rows * n_row),
        out_shape=(
            jax.ShapeDtypeStruct((cols, rows), f32),
            jax.ShapeDtypeStruct((queries // LANES, LANES), f32),
        ),
        in_specs=[hbm] * 4,
        out_specs=(vmem, vmem),
        scratch_shapes=[
            pltpu.VMEM((rows, cols), f32),
            pltpu.VMEM((3, queries), jnp.int32),
            pltpu.VMEM((3, queries), jnp.int32),
            pltpu.VMEM((queries // LANES, LANES), f32),
            pltpu.VMEM((cols, rows), f32),
            pltpu.VMEM((cols, rows), f32),
            pltpu.VMEM((2 * rows, half_c), bf16),
            pltpu.VMEM((half_c, 3 * queries), bf16),
            pltpu.VMEM((rows, 3 * queries), f32),
            pltpu.VMEM((2 * rows, 3 * queries), bf16),
            pltpu.VMEM((2, n_row, queries // 2 // LANES, LANES), f32),
            pltpu.VMEM((2, 2, half_c, rows), f32),
            pltpu.VMEM((half_c, rows), f32),
            pltpu.VMEM((PARTS, n_z, half_c // n_piece, rows), f32),
            dma((5,)), dma((2,)), dma((5,)), dma((n_piece,)), dma((PARTS,)), dma((PARTS, n_z)), dma((1,)),
        ],
        compiler_params=pltpu.CompilerParams(
            collective_id=0, has_side_effects=True, vmem_limit_bytes=VMEM_BYTES
        ),
    )(*(pltpu.with_memory_space_constraint(a, pltpu.HBM) for a in given))
    new_rows, residual = pl.pallas_call(
        finish,
        out_shape=(
            jax.ShapeDtypeStruct((rows, cols), jnp.float32),
            jax.ShapeDtypeStruct((queries // LANES, LANES), jnp.float32),
        ),
        in_specs=[vmem, vmem],
        out_specs=(vmem, vmem),
        compiler_params=pltpu.CompilerParams(vmem_limit_bytes=4 * 1024 * 1024),
    )(tall, misfit)
    return new_rows, residual.reshape(queries)


def solution(mesh):
    placed = (P("row", None), P(None, "query"), P(None, "query"), P("query"))
    return jax.shard_map(
        functools.partial(local, mesh.shape["row"], mesh.shape["query"]),
        mesh=mesh, in_specs=placed, out_specs=(P("row", None), P("query")), check_vma=False,
    )
```

```python
import functools

import jax
import jax.numpy as jnp
from jax import lax
from jax.experimental import pallas as pl
from jax.experimental.pallas import tpu as pltpu
from jax.sharding import PartitionSpec as P

VALS = 16
STEP_RATE = 2.0
CHUNK = 256
PARTS = 2
LOADS = 4
VMEM_BYTES = 48 * 1024 * 1024
LANES = 128
BLOCK = 256
PACK = 256
MESH = pl.DeviceIdType.MESH


def group_softmax(tall):
    cols, rows = tall.shape
    grouped = tall.reshape(cols // VALS, VALS, rows)
    shifted = jnp.exp(grouped - jnp.max(grouped, axis=1, keepdims=True))
    return (shifted / jnp.sum(shifted, axis=1, keepdims=True)).reshape(cols, rows)


def kernel(
    n_row, n_query, total_rows,
    log_hbm, att_hbm, val_hbm, tgt_hbm, gat, res_ref,
    log_v, att, val, tgt, log_t, rel_t, rel_b, sel, pair, wgt, ans, acc, sib, zin,
    load_sem, ans_recv, send_sem, sib_recv, z_recv, ag_recv, fw_recv,
):
    me_r = lax.axis_index("row")
    me_q = lax.axis_index("query")
    me_z, core = me_q // 2, me_q % 2
    other = 1 - core
    n_z = n_query // 2
    rows, cols = log_hbm.shape
    queries = att.shape[1]
    half_q = queries // 2
    half_c = cols // 2
    share = half_c // n_z
    size = share // PARTS
    n_block = half_c // BLOCK
    lower = me_z < n_z // 2
    sibling = (me_r, me_z * 2 + other)

    def remote(src, dst, ssem, rsem, device):
        return pltpu.make_async_remote_copy(
            src_ref=src, dst_ref=dst, send_sem=ssem, recv_sem=rsem,
            device_id=device, device_id_type=MESH,
        )

    small = [
        pltpu.make_async_copy(att_hbm, att, load_sem.at[2]),
        pltpu.make_async_copy(val_hbm, val, load_sem.at[3]),
        pltpu.make_async_copy(tgt_hbm, tgt, load_sem.at[4]),
    ]
    band = rows // LOADS
    wide = cols // 2
    large = [
        pltpu.make_async_copy(
            log_hbm.at[b * band : (b + 1) * band, side * wide : (side + 1) * wide],
            log_v.at[b * band : (b + 1) * band, side * wide : (side + 1) * wide], load_sem.at[side],
        )
        for side in range(2) for b in range(LOADS)
    ]
    for copy in large + small:
        copy.start()

    barrier = pltpu.get_barrier_semaphore()
    for d in range(1, n_row):
        pl.semaphore_signal(barrier, inc=1, device_id=(lax.rem(me_r + d, n_row), me_q), device_id_type=MESH)
    pl.semaphore_signal(barrier, inc=1, device_id=sibling, device_id_type=MESH)
    for d in range(1, n_z):
        pl.semaphore_signal(
            barrier, inc=1, device_id=(me_r, lax.rem(me_z + d, n_z) * 2 + core), device_id_type=MESH
        )

    for b in range(cols // LANES):
        if b * LANES % wide == 0:
            side = b * LANES // wide
            half_v = log_v.at[:, side * wide : (side + 1) * wide]
            pltpu.make_async_copy(half_v, half_v, load_sem.at[side]).wait()
        part = slice(b * LANES, (b + 1) * LANES)
        tall = log_v[:, part].T
        log_t[part, :] = tall
        relaxed = group_softmax(tall)
        rel_t[part, :] = relaxed
        side, inside = divmod(b * LANES, half_c)
        rel_b[side * rows : (side + 1) * rows, inside : inside + LANES] = relaxed.T.astype(jnp.bfloat16)
    for copy in small:
        copy.wait()

    places = lax.broadcasted_iota(jnp.int32, (PACK, CHUNK), 0).astype(jnp.float32).astype(jnp.bfloat16)
    one, zero = jnp.ones((), jnp.bfloat16), jnp.zeros((), jnp.bfloat16)
    chunks = half_q // CHUNK

    def ans_copy(h, d, slot):
        dst = (lax.rem(me_r + d, n_row), me_q)
        return remote(ans.at[h, slot], ans.at[h, slot], send_sem.at[4], ans_recv.at[h], dst)

    for h in range(2):

        def forward(c, carry, h=h):
            at = h * half_q + c * CHUNK
            base = at * 3
            picked = []
            for k in range(3):
                column = att[k : k + 1, pl.ds(at, CHUNK)] * VALS + val[k : k + 1, pl.ds(at, CHUNK)]
                high = column >= half_c
                low = jnp.where(high, column - half_c, column).astype(jnp.float32)
                parts = []
                for s in range(half_c // PACK):
                    index = jnp.broadcast_to(low - float(s * PACK), (PACK, CHUNK)).astype(jnp.bfloat16)
                    one_hot = jnp.where(places == index, one, zero)
                    sel[s * PACK : (s + 1) * PACK, pl.ds(base + k * CHUNK, CHUNK)] = one_hot
                    parts.append(one_hot)
                both = jnp.dot(rel_b[...], jnp.concatenate(parts, axis=0), preferred_element_type=jnp.float32)
                picked.append(jnp.where(high, both[rows:, :], both[:rows, :]))
            first = picked[0] * picked[1]
            pair[:, pl.ds(base, CHUNK)] = picked[1] * picked[2]
            pair[:, pl.ds(base + CHUNK, CHUNK)] = picked[0] * picked[2]
            pair[:, pl.ds(base + 2 * CHUNK, CHUNK)] = first
            partial = jnp.sum(first * picked[2], axis=0, keepdims=True)
            for i in range(CHUNK // LANES):
                ans[h, me_r, pl.ds(c * (CHUNK // LANES) + i, 1), :] = partial[:, i * LANES : (i + 1) * LANES]
            return carry

        for c in range(chunks):
            forward(c, 0)
        if h == 0:
            pl.semaphore_wait(barrier, n_row - 1 + n_z)
        for d in range(1, n_row):
            ans_copy(h, d, me_r).start()

    answer_scale = float(VALS**3) / total_rows
    half_lines = half_q // LANES

    def sums(block, h):
        span = slice(h * 3 * half_q, (h + 1) * 3 * half_q)
        return lax.dot_general(
            sel[block * BLOCK : (block + 1) * BLOCK, span], wgt[:, span], (((1,), (1,)), ((), ())),
            preferred_element_type=jnp.float32,
        )

    def at(p):
        return pl.ds(pl.multiple_of(p * size, size), size)

    def own(p):
        return pl.ds(pl.multiple_of(core * half_c + p * size, size), size)

    def theirs(p):
        return pl.ds(pl.multiple_of(other * half_c + p * size, size), size)

    def outward(i):
        return (i + 1) % n_z

    def sib_copy(p):
        return remote(acc.at[0, other, at(p)], sib.at[at(p)], send_sem.at[0], sib_recv.at[p], sibling)

    def z_copy(part, dst_z, slot):
        return remote(
            acc.at[0, core, at(part * n_z + dst_z)], zin.at[part, slot], send_sem.at[1], z_recv.at[part],
            (me_r, dst_z * 2 + core),
        )

    def ag_copy(part, dst_z, z):
        span = own(part * n_z + z)
        return remote(gat.at[span], gat.at[span], send_sem.at[2], ag_recv.at[part, z], (me_r, dst_z * 2 + core))

    def fw_copy(p, mine):
        span = own(p) if mine else theirs(p)
        return remote(gat.at[span], gat.at[span], send_sem.at[3], fw_recv.at[0], sibling)

    def toward(d):
        return lax.rem(me_z + jnp.where(lower, 1, n_z - 1) * d, n_z)

    def spread(part):
        for i in range(n_z):
            z = outward(i)
            p = part * n_z + z
            sib_copy(p).wait_recv()
            summed = acc[0, core, at(p)] + sib[at(p)]

            @pl.when(z != me_z)
            def _():
                acc[0, core, at(p)] = summed
                z_copy(part, z, me_z).start()

            @pl.when(z == me_z)
            def _():
                zin[part, me_z] = summed

    def reduce(part):
        remote(zin.at[part, 1:], zin.at[part, 1:], send_sem.at[1], z_recv.at[part], sibling).wait_recv()
        accumulated = zin[part, 0]
        for z in range(1, n_z):
            accumulated = accumulated + zin[part, z]
        mine = own(part * n_z + me_z)
        groups = size // VALS
        grouped_d = (float(VALS * VALS) * accumulated).reshape(groups, VALS, rows)
        grouped_p = rel_t[mine, :].reshape(groups, VALS, rows)
        weighted_mean = jnp.sum(grouped_p * grouped_d, axis=1, keepdims=True)
        tangent = (grouped_p * (grouped_d - weighted_mean)).reshape(size, rows)
        gat[mine, :] = group_softmax(log_t[mine, :] - STEP_RATE * tangent)
        @pl.when(me_z != 0)
        def _():
            ag_copy(part, 0, me_z).start()

        @pl.when(me_z == 0)
        def _():
            for z in range(1, n_z):
                ag_copy(part, z, 0).start()

        fw_copy(part * n_z + me_z, True).start()

    def relay(part):
        for d in range(1, n_z):
            z = toward(d)
            ag_copy(part, z, z).wait_recv()
            fw_copy(part * n_z + z, True).start()

    for h in range(2):
        remote(ans.at[h, 1:], ans.at[h, 1:], send_sem.at[4], ans_recv.at[h], sibling).wait_recv()
        total = ans[h, 0]
        for r in range(1, n_row):
            total = total + ans[h, r]
        lines = slice(h * half_lines, (h + 1) * half_lines)
        residual = total * answer_scale - tgt[lines, :]
        res_ref[lines, :] = residual
        for line in range(half_lines):
            chunk, inside = divmod(line * LANES, CHUNK)
            misfit = residual[line : line + 1, :]
            for k in range(3):
                start = h * 3 * half_q + (chunk * 3 + k) * CHUNK + inside
                span = slice(start, start + LANES)
                query = h * half_q + line * LANES
                high = att[k : k + 1, query : query + LANES] >= half_c // VALS
                product = pair[:, span]
                wgt[:rows, span] = (product * jnp.where(high, 0.0, misfit)).astype(jnp.bfloat16)
                wgt[rows:, span] = (product * jnp.where(high, misfit, 0.0)).astype(jnp.bfloat16)
        for block in range(n_block):
            found = sums(block, h)
            span = slice(block * BLOCK, (block + 1) * BLOCK)
            acc[h, 0, span] = found[:, :rows]
            acc[h, 1, span] = found[:, rows:]
    for side in range(2):
        acc[0, side] = acc[0, side] + acc[1, side]
    for part in range(PARTS):
        for i in range(n_z):
            sib_copy(part * n_z + outward(i)).start()
    for part in range(PARTS):
        spread(part)
    for part in range(PARTS):
        reduce(part)
    for part in range(PARTS):
        for z in range(1, n_z):
            @pl.when(jnp.logical_and(me_z != 0, z != me_z))
            def _():
                ag_copy(part, z, me_z).start()
    for part in range(PARTS):
        relay(part)
    half = gat.at[pl.ds(0, half_c)]
    remote(half, half, send_sem.at[3], fw_recv.at[0], sibling).wait_recv()

    remote(ans.at[:, 1:], ans.at[:, 1:], send_sem.at[4], ans_recv.at[0], sibling).wait_send()

    def sent(many, sem):
        span = pl.ds(0, many * share)
        remote(acc.at[0, 0, span], acc.at[0, 0, span], send_sem.at[sem], sib_recv.at[0], sibling).wait_send()

    sent(n_z, 0)
    sent(n_z - 1, 1)
    sent(n_z - 1, 2)
    sent(n_z, 3)

def finish(tall_ref, misfit_ref, new_ref, res_ref):
    for b in range(tall_ref.shape[0] // LANES):
        part = slice(b * LANES, (b + 1) * LANES)
        new_ref[:, part] = tall_ref[part, :].T
    res_ref[...] = misfit_ref[...]


def local(n_row, n_query, logits, attributes, values, targets):
    rows, cols = logits.shape
    queries = attributes.shape[1]
    half_c = cols // 2
    n_z = n_query // 2
    n_piece = n_z * PARTS
    dma = pltpu.SemaphoreType.DMA
    vmem = pl.BlockSpec(memory_space=pltpu.VMEM)
    hbm = pl.BlockSpec(memory_space=pltpu.HBM)
    f32, bf16 = jnp.float32, jnp.bfloat16
    given = (logits, attributes, values, targets.reshape(queries // LANES, LANES))
    tall, misfit = pl.pallas_call(
        functools.partial(kernel, n_row, n_query, rows * n_row),
        out_shape=(
            jax.ShapeDtypeStruct((cols, rows), f32),
            jax.ShapeDtypeStruct((queries // LANES, LANES), f32),
        ),
        in_specs=[hbm] * 4,
        out_specs=(vmem, vmem),
        scratch_shapes=[
            pltpu.VMEM((rows, cols), f32),
            pltpu.VMEM((3, queries), jnp.int32),
            pltpu.VMEM((3, queries), jnp.int32),
            pltpu.VMEM((queries // LANES, LANES), f32),
            pltpu.VMEM((cols, rows), f32),
            pltpu.VMEM((cols, rows), f32),
            pltpu.VMEM((2 * rows, half_c), bf16),
            pltpu.VMEM((half_c, 3 * queries), bf16),
            pltpu.VMEM((rows, 3 * queries), f32),
            pltpu.VMEM((2 * rows, 3 * queries), bf16),
            pltpu.VMEM((2, n_row, queries // 2 // LANES, LANES), f32),
            pltpu.VMEM((2, 2, half_c, rows), f32),
            pltpu.VMEM((half_c, rows), f32),
            pltpu.VMEM((PARTS, n_z, half_c // n_piece, rows), f32),
            dma((5,)), dma((2,)), dma((5,)), dma((n_piece,)), dma((PARTS,)), dma((PARTS, n_z)), dma((1,)),
        ],
        compiler_params=pltpu.CompilerParams(
            collective_id=0, has_side_effects=True, vmem_limit_bytes=VMEM_BYTES
        ),
    )(*(pltpu.with_memory_space_constraint(a, pltpu.HBM) for a in given))
    new_rows, residual = pl.pallas_call(
        finish,
        out_shape=(
            jax.ShapeDtypeStruct((rows, cols), jnp.float32),
            jax.ShapeDtypeStruct((queries // LANES, LANES), jnp.float32),
        ),
        in_specs=[vmem, vmem],
        out_specs=(vmem, vmem),
        compiler_params=pltpu.CompilerParams(vmem_limit_bytes=4 * 1024 * 1024),
    )(tall, misfit)
    return new_rows, residual.reshape(queries)


def solution(mesh):
    placed = (P("row", None), P(None, "query"), P(None, "query"), P("query"))
    return jax.shard_map(
        functools.partial(local, mesh.shape["row"], mesh.shape["query"]),
        mesh=mesh, in_specs=placed, out_specs=(P("row", None), P("query")), check_vma=False,
    )
```

```python
import functools

import jax
import jax.numpy as jnp
from jax import lax
from jax.experimental import pallas as pl
from jax.experimental.pallas import tpu as pltpu
from jax.sharding import PartitionSpec as P

VALS = 16
STEP_RATE = 2.0
CHUNK = 256
PARTS = 4
LOADS = 4
VMEM_BYTES = 48 * 1024 * 1024
LANES = 128
BLOCK = 256
PACK = 256
MESH = pl.DeviceIdType.MESH


def group_softmax(tall):
    cols, rows = tall.shape
    grouped = tall.reshape(cols // VALS, VALS, rows)
    shifted = jnp.exp(grouped - jnp.max(grouped, axis=1, keepdims=True))
    return (shifted / jnp.sum(shifted, axis=1, keepdims=True)).reshape(cols, rows)


def kernel(
    n_row, n_query, total_rows,
    log_hbm, att_hbm, val_hbm, tgt_hbm, gat, res_ref,
    log_v, att, val, tgt, log_t, rel_t, rel_b, sel, pair, wgt, ans, acc, sib, zin,
    load_sem, ans_recv, send_sem, sib_recv, z_recv, ag_recv, fw_recv,
):
    me_r = lax.axis_index("row")
    me_q = lax.axis_index("query")
    me_z, core = me_q // 2, me_q % 2
    other = 1 - core
    n_z = n_query // 2
    rows, cols = log_hbm.shape
    queries = att.shape[1]
    half_q = queries // 2
    half_c = cols // 2
    share = half_c // n_z
    size = share // PARTS
    n_block = half_c // BLOCK
    lower = me_z < n_z // 2
    sibling = (me_r, me_z * 2 + other)

    def remote(src, dst, ssem, rsem, device):
        return pltpu.make_async_remote_copy(
            src_ref=src, dst_ref=dst, send_sem=ssem, recv_sem=rsem,
            device_id=device, device_id_type=MESH,
        )

    small = [
        pltpu.make_async_copy(att_hbm, att, load_sem.at[2]),
        pltpu.make_async_copy(val_hbm, val, load_sem.at[3]),
        pltpu.make_async_copy(tgt_hbm, tgt, load_sem.at[4]),
    ]
    band = rows // LOADS
    wide = cols // 2
    large = [
        pltpu.make_async_copy(
            log_hbm.at[b * band : (b + 1) * band, side * wide : (side + 1) * wide],
            log_v.at[b * band : (b + 1) * band, side * wide : (side + 1) * wide], load_sem.at[side],
        )
        for side in range(2) for b in range(LOADS)
    ]
    for copy in large + small:
        copy.start()

    barrier = pltpu.get_barrier_semaphore()
    for d in range(1, n_row):
        pl.semaphore_signal(barrier, inc=1, device_id=(lax.rem(me_r + d, n_row), me_q), device_id_type=MESH)
    pl.semaphore_signal(barrier, inc=1, device_id=sibling, device_id_type=MESH)
    for d in range(1, n_z):
        pl.semaphore_signal(
            barrier, inc=1, device_id=(me_r, lax.rem(me_z + d, n_z) * 2 + core), device_id_type=MESH
        )

    for b in range(cols // LANES):
        if b * LANES % wide == 0:
            side = b * LANES // wide
            half_v = log_v.at[:, side * wide : (side + 1) * wide]
            pltpu.make_async_copy(half_v, half_v, load_sem.at[side]).wait()
        part = slice(b * LANES, (b + 1) * LANES)
        tall = log_v[:, part].T
        log_t[part, :] = tall
        relaxed = group_softmax(tall)
        rel_t[part, :] = relaxed
        side, inside = divmod(b * LANES, half_c)
        rel_b[side * rows : (side + 1) * rows, inside : inside + LANES] = relaxed.T.astype(jnp.bfloat16)
    for copy in small:
        copy.wait()

    places = lax.broadcasted_iota(jnp.int32, (PACK, CHUNK), 0).astype(jnp.float32).astype(jnp.bfloat16)
    one, zero = jnp.ones((), jnp.bfloat16), jnp.zeros((), jnp.bfloat16)
    chunks = half_q // CHUNK

    def ans_copy(h, d, slot):
        dst = (lax.rem(me_r + d, n_row), me_q)
        return remote(ans.at[h, slot], ans.at[h, slot], send_sem.at[4], ans_recv.at[h], dst)

    for h in range(2):

        def forward(c, carry, h=h):
            at = h * half_q + c * CHUNK
            base = at * 3
            picked = []
            for k in range(3):
                column = att[k : k + 1, pl.ds(at, CHUNK)] * VALS + val[k : k + 1, pl.ds(at, CHUNK)]
                high = column >= half_c
                low = jnp.where(high, column - half_c, column).astype(jnp.float32)
                parts = []
                for s in range(half_c // PACK):
                    index = jnp.broadcast_to(low - float(s * PACK), (PACK, CHUNK)).astype(jnp.bfloat16)
                    one_hot = jnp.where(places == index, one, zero)
                    sel[s * PACK : (s + 1) * PACK, pl.ds(base + k * CHUNK, CHUNK)] = one_hot
                    parts.append(one_hot)
                both = jnp.dot(rel_b[...], jnp.concatenate(parts, axis=0), preferred_element_type=jnp.float32)
                picked.append(jnp.where(high, both[rows:, :], both[:rows, :]))
            first = picked[0] * picked[1]
            pair[:, pl.ds(base, CHUNK)] = picked[1] * picked[2]
            pair[:, pl.ds(base + CHUNK, CHUNK)] = picked[0] * picked[2]
            pair[:, pl.ds(base + 2 * CHUNK, CHUNK)] = first
            partial = jnp.sum(first * picked[2], axis=0, keepdims=True)
            for i in range(CHUNK // LANES):
                ans[h, me_r, pl.ds(c * (CHUNK // LANES) + i, 1), :] = partial[:, i * LANES : (i + 1) * LANES]
            return carry

        for c in range(chunks):
            forward(c, 0)
        if h == 0:
            pl.semaphore_wait(barrier, n_row - 1 + n_z)
        for d in range(1, n_row):
            ans_copy(h, d, me_r).start()

    answer_scale = float(VALS**3) / total_rows
    half_lines = half_q // LANES

    def sums(block, h):
        span = slice(h * 3 * half_q, (h + 1) * 3 * half_q)
        return lax.dot_general(
            sel[block * BLOCK : (block + 1) * BLOCK, span], wgt[:, span], (((1,), (1,)), ((), ())),
            preferred_element_type=jnp.float32,
        )

    def at(p):
        return pl.ds(pl.multiple_of(p * size, size), size)

    def own(p):
        return pl.ds(pl.multiple_of(core * half_c + p * size, size), size)

    def theirs(p):
        return pl.ds(pl.multiple_of(other * half_c + p * size, size), size)

    def outward(i):
        return (i + 1) % n_z

    def sib_copy(p):
        return remote(acc.at[0, other, at(p)], sib.at[at(p)], send_sem.at[0], sib_recv.at[p], sibling)

    def z_copy(part, dst_z, slot):
        return remote(
            acc.at[0, core, at(part * n_z + dst_z)], zin.at[part, slot], send_sem.at[1], z_recv.at[part],
            (me_r, dst_z * 2 + core),
        )

    def ag_copy(part, dst_z, z):
        span = own(part * n_z + z)
        return remote(gat.at[span], gat.at[span], send_sem.at[2], ag_recv.at[part, z], (me_r, dst_z * 2 + core))

    def fw_copy(p, mine):
        span = own(p) if mine else theirs(p)
        return remote(gat.at[span], gat.at[span], send_sem.at[3], fw_recv.at[0], sibling)

    def toward(d):
        return lax.rem(me_z + jnp.where(lower, 1, n_z - 1) * d, n_z)

    def spread(part):
        for i in range(n_z):
            z = outward(i)
            p = part * n_z + z
            sib_copy(p).wait_recv()
            summed = acc[0, core, at(p)] + sib[at(p)]

            @pl.when(z != me_z)
            def _():
                acc[0, core, at(p)] = summed
                z_copy(part, z, me_z).start()

            @pl.when(z == me_z)
            def _():
                zin[part, me_z] = summed

    def reduce(part):
        remote(zin.at[part, 1:], zin.at[part, 1:], send_sem.at[1], z_recv.at[part], sibling).wait_recv()
        accumulated = zin[part, 0]
        for z in range(1, n_z):
            accumulated = accumulated + zin[part, z]
        mine = own(part * n_z + me_z)
        groups = size // VALS
        grouped_d = (float(VALS * VALS) * accumulated).reshape(groups, VALS, rows)
        grouped_p = rel_t[mine, :].reshape(groups, VALS, rows)
        weighted_mean = jnp.sum(grouped_p * grouped_d, axis=1, keepdims=True)
        tangent = (grouped_p * (grouped_d - weighted_mean)).reshape(size, rows)
        gat[mine, :] = group_softmax(log_t[mine, :] - STEP_RATE * tangent)
        @pl.when(me_z != 0)
        def _():
            ag_copy(part, 0, me_z).start()

        @pl.when(me_z == 0)
        def _():
            for z in range(1, n_z):
                ag_copy(part, z, 0).start()

        fw_copy(part * n_z + me_z, True).start()

    def relay(part):
        for d in range(1, n_z):
            z = toward(d)
            ag_copy(part, z, z).wait_recv()
            fw_copy(part * n_z + z, True).start()

    for h in range(2):
        remote(ans.at[h, 1:], ans.at[h, 1:], send_sem.at[4], ans_recv.at[h], sibling).wait_recv()
        total = ans[h, 0]
        for r in range(1, n_row):
            total = total + ans[h, r]
        lines = slice(h * half_lines, (h + 1) * half_lines)
        residual = total * answer_scale - tgt[lines, :]
        res_ref[lines, :] = residual
        for line in range(half_lines):
            chunk, inside = divmod(line * LANES, CHUNK)
            misfit = residual[line : line + 1, :]
            for k in range(3):
                start = h * 3 * half_q + (chunk * 3 + k) * CHUNK + inside
                span = slice(start, start + LANES)
                query = h * half_q + line * LANES
                high = att[k : k + 1, query : query + LANES] >= half_c // VALS
                product = pair[:, span]
                wgt[:rows, span] = (product * jnp.where(high, 0.0, misfit)).astype(jnp.bfloat16)
                wgt[rows:, span] = (product * jnp.where(high, misfit, 0.0)).astype(jnp.bfloat16)
        for block in range(n_block):
            found = sums(block, h)
            span = slice(block * BLOCK, (block + 1) * BLOCK)
            acc[h, 0, span] = found[:, :rows]
            acc[h, 1, span] = found[:, rows:]
    for side in range(2):
        acc[0, side] = acc[0, side] + acc[1, side]
    for part in range(PARTS):
        for i in range(n_z):
            sib_copy(part * n_z + outward(i)).start()
    for part in range(PARTS):
        spread(part)
    for part in range(PARTS):
        reduce(part)
    for part in range(PARTS):
        for z in range(1, n_z):
            @pl.when(jnp.logical_and(me_z != 0, z != me_z))
            def _():
                ag_copy(part, z, me_z).start()
    for part in range(PARTS):
        relay(part)
    half = gat.at[pl.ds(0, half_c)]
    remote(half, half, send_sem.at[3], fw_recv.at[0], sibling).wait_recv()

    remote(ans.at[:, 1:], ans.at[:, 1:], send_sem.at[4], ans_recv.at[0], sibling).wait_send()

    def sent(many, sem):
        span = pl.ds(0, many * share)
        remote(acc.at[0, 0, span], acc.at[0, 0, span], send_sem.at[sem], sib_recv.at[0], sibling).wait_send()

    sent(n_z, 0)
    sent(n_z - 1, 1)
    sent(n_z - 1, 2)
    sent(n_z, 3)

def finish(tall_ref, misfit_ref, new_ref, res_ref):
    for b in range(tall_ref.shape[0] // LANES):
        part = slice(b * LANES, (b + 1) * LANES)
        new_ref[:, part] = tall_ref[part, :].T
    res_ref[...] = misfit_ref[...]


def local(n_row, n_query, logits, attributes, values, targets):
    rows, cols = logits.shape
    queries = attributes.shape[1]
    half_c = cols // 2
    n_z = n_query // 2
    n_piece = n_z * PARTS
    dma = pltpu.SemaphoreType.DMA
    vmem = pl.BlockSpec(memory_space=pltpu.VMEM)
    hbm = pl.BlockSpec(memory_space=pltpu.HBM)
    f32, bf16 = jnp.float32, jnp.bfloat16
    given = (logits, attributes, values, targets.reshape(queries // LANES, LANES))
    tall, misfit = pl.pallas_call(
        functools.partial(kernel, n_row, n_query, rows * n_row),
        out_shape=(
            jax.ShapeDtypeStruct((cols, rows), f32),
            jax.ShapeDtypeStruct((queries // LANES, LANES), f32),
        ),
        in_specs=[hbm] * 4,
        out_specs=(vmem, vmem),
        scratch_shapes=[
            pltpu.VMEM((rows, cols), f32),
            pltpu.VMEM((3, queries), jnp.int32),
            pltpu.VMEM((3, queries), jnp.int32),
            pltpu.VMEM((queries // LANES, LANES), f32),
            pltpu.VMEM((cols, rows), f32),
            pltpu.VMEM((cols, rows), f32),
            pltpu.VMEM((2 * rows, half_c), bf16),
            pltpu.VMEM((half_c, 3 * queries), bf16),
            pltpu.VMEM((rows, 3 * queries), f32),
            pltpu.VMEM((2 * rows, 3 * queries), bf16),
            pltpu.VMEM((2, n_row, queries // 2 // LANES, LANES), f32),
            pltpu.VMEM((2, 2, half_c, rows), f32),
            pltpu.VMEM((half_c, rows), f32),
            pltpu.VMEM((PARTS, n_z, half_c // n_piece, rows), f32),
            dma((5,)), dma((2,)), dma((5,)), dma((n_piece,)), dma((PARTS,)), dma((PARTS, n_z)), dma((1,)),
        ],
        compiler_params=pltpu.CompilerParams(
            collective_id=0, has_side_effects=True, vmem_limit_bytes=VMEM_BYTES
        ),
    )(*(pltpu.with_memory_space_constraint(a, pltpu.HBM) for a in given))
    new_rows, residual = pl.pallas_call(
        finish,
        out_shape=(
            jax.ShapeDtypeStruct((rows, cols), jnp.float32),
            jax.ShapeDtypeStruct((queries // LANES, LANES), jnp.float32),
        ),
        in_specs=[vmem, vmem],
        out_specs=(vmem, vmem),
        compiler_params=pltpu.CompilerParams(vmem_limit_bytes=4 * 1024 * 1024),
    )(tall, misfit)
    return new_rows, residual.reshape(queries)


def solution(mesh):
    placed = (P("row", None), P(None, "query"), P(None, "query"), P("query"))
    return jax.shard_map(
        functools.partial(local, mesh.shape["row"], mesh.shape["query"]),
        mesh=mesh, in_specs=placed, out_specs=(P("row", None), P("query")), check_vma=False,
    )
```
